32 devices in a mesh: dir: 16 (over z, y, x), box: 2 (over core).
Axes of the slice: x: 2, y: 2, z: 4, core: 2. Of those that a mesh axis runs over, the one named last changes fastest.
Arguments:
- child_fields: bfloat16 [256, 8, 2, 512], P(('box', 'dir')), may hold values from -6 to 6
- interp_matrix: bfloat16 [512, 2048], replicated, may hold values from -0.25 to 0.25
- phase_angle: float32 [8, 2048], replicated, may hold values from -3.140625 to 3.140625
- patch_order: int32 [2, 128], P('box'), may hold values from 0 to 127, each once within a row
- offset_code: int32 [16, 16, 40], P('box'), may hold values from 0 to 48
- operator_index: int32 [16, 16, 40], P('box'), may hold values from 0 to 127
- operators: bfloat16 [128, 2, 2048], P(None, None, 'dir'), may hold values from -1 to 1
Outputs:
- local_fields: bfloat16 [256, 8, 2, 512], P(('box', 'dir'))
The draws below stay inside these ranges and needn't reach their ends.
Inputs may be any that keep to these rules, and one draw needn't show every extreme that they name: `patch_order`: each row holds every number of 0 to 127 once. `offset_code`: entry a names the box offset (a // 7 - 3, a % 7 - 3) on the surface grid, whose two dimensions wrap around.
All inputs are finite; a program needn't handle non-finite values.
Results may differ from the reference program's by a relative error of at most 0.0064.
Values may be sent and summed in bfloat16 or wider, within the bound.
A program may use at most 64 MiB of HBM per device.

```python
import math
import jax
import jax.numpy as jnp
from jax import lax

DC = 512
DP = 2048
CHILDREN = 8
NLIST = 40
NOPS = 128
PV = 16
PB = 128
NPATCH = 2
NU = 16
BOXES = 256


def place_ends(values, rng, low, high):
    index_at = [jax.random.randint(jax.random.fold_in(rng, axis), (), 0, length) for axis, length in enumerate(values.shape)]
    main_axis = values.shape.index(max(values.shape))
    neighbour = index_at[:main_axis] + [(index_at[main_axis] + 1) % values.shape[main_axis]] + index_at[main_axis + 1:]
    return values.at[tuple(index_at)].set(low).at[tuple(neighbour)].set(high)


def block_levels(own_key, extent, split, smallest, top_value):
    factor_of = 1.0
    for axis_at, parts in split:
        steps = jax.random.uniform(jax.random.fold_in(jax.random.fold_in(own_key, 6), axis_at), (parts,), jnp.float32, smallest / len(split), top_value / len(split))
        factor_of = factor_of * jnp.repeat(jnp.exp(steps), extent[axis_at] // parts).reshape((-1,) + (1,) * (len(extent) - 1 - axis_at))
    return factor_of


def gaussian(rng, shape, width, limit, pieces=(), held_as=jnp.bfloat16):
    factor_of = block_levels(rng, shape, pieces, -0.22, 0.18) if pieces else 1.0
    array = jax.random.normal(rng, shape, jnp.float32) * width * factor_of
    return jnp.minimum(jnp.maximum(array, -limit), limit).astype(held_as)


def setup_inputs(seed: int = 0) -> dict:
    arg_keys = jax.random.split(jax.random.key(seed), 8)
    child_fields = gaussian(arg_keys[0], (BOXES, CHILDREN, 2, DC), 1.0, 6.0, ((0, 32),))
    interp_matrix = gaussian(arg_keys[1], (DC, DP), DC ** -0.5, 0.25)
    phase_angle = jnp.clip(jax.random.uniform(arg_keys[2], (CHILDREN, DP), jnp.float32, -3.140625, 3.140625), -3.140625, 3.140625)
    patch_order = jax.vmap(lambda own: jax.random.permutation(own, PB))(jax.random.split(arg_keys[3], NPATCH)).reshape((NPATCH, PB)).astype(jnp.int32)
    offset_code = place_ends(jax.random.randint(arg_keys[4], (NU, PV, NLIST), 0, 49), jax.random.fold_in(arg_keys[4], 1), 0, 48).astype(jnp.int32)
    operator_index = place_ends(jax.random.randint(arg_keys[5], (NU, PV, NLIST), 0, NOPS), jax.random.fold_in(arg_keys[5], 1), 0, NOPS - 1).astype(jnp.int32)
    operators = gaussian(arg_keys[6], (NOPS, 2, DP), NLIST ** -0.5, 1.0, ((2, 16),))
    return {"child_fields": child_fields, "interp_matrix": interp_matrix, "phase_angle": phase_angle, "patch_order": patch_order, "offset_code": offset_code, "operator_index": operator_index, "operators": operators}


def aggregate_boxes(fields, interp_matrix, cosine_part, sine_part):
    box_count = fields.shape[0]
    flat_rows = fields.reshape(box_count * CHILDREN * 2, DC)
    product = jnp.dot(flat_rows, interp_matrix, preferred_element_type=jnp.float32).reshape(box_count, CHILDREN, 2, DP)
    real_part = jnp.sum(cosine_part * product[:, :, 0] - sine_part * product[:, :, 1], axis=1)
    imaginary_component = jnp.sum(cosine_part * product[:, :, 1] + sine_part * product[:, :, 0], axis=1)
    return jnp.stack([real_part, imaginary_component], axis=1).astype(jnp.bfloat16)


def anterpolate_boxes(fields, interp_matrix, cosine_part, sine_part):
    box_count = fields.shape[0]
    values = fields.astype(jnp.float32)
    shifted_real = cosine_part * values[:, None, 0] + sine_part * values[:, None, 1]
    shifted_imag = cosine_part * values[:, None, 1] - sine_part * values[:, None, 0]
    shifted = jnp.stack([shifted_real, shifted_imag], axis=2).astype(jnp.bfloat16)
    flat_rows = shifted.reshape(box_count * CHILDREN * 2, DP)
    result = lax.dot_general(flat_rows, interp_matrix, (((1,), (1,)), ((), ())), preferred_element_type=jnp.float32)
    return (result * (DC / DP)).astype(jnp.bfloat16).reshape(box_count, CHILDREN, 2, DC)


def translate_band(grid, codes, chosen, ops_band):
    row_ids = jnp.arange(NU, dtype=jnp.int32)[:, None]
    col_ids = jnp.arange(PV, dtype=jnp.int32)[None, :]
    band_width = grid.shape[3]

    def accumulate(totals, inputs):
        entry_code, entry_operator = inputs
        source_row = (row_ids + entry_code // 7 - 3) % NU
        source_col = (col_ids + entry_code % 7 - 3) % PV
        source = grid[source_row, source_col].astype(jnp.float32)
        factor = ops_band[entry_operator].astype(jnp.float32)
        real_total = totals[0] + factor[:, :, 0] * source[:, :, 0] - factor[:, :, 1] * source[:, :, 1]
        imag_total = totals[1] + factor[:, :, 0] * source[:, :, 1] + factor[:, :, 1] * source[:, :, 0]
        return (real_total, imag_total), None

    empty_total = jnp.zeros((NU, PV, band_width), jnp.float32)
    totals, unused = lax.scan(accumulate, (empty_total, empty_total), (codes, chosen))
    return jnp.stack([totals[0], totals[1]], axis=2).astype(jnp.bfloat16)


def reference(child_fields, interp_matrix, phase_angle, patch_order, offset_code, operator_index, operators):
    cosine_part = jnp.cos(phase_angle)
    sine_part = jnp.sin(phase_angle)
    block_boxes = math.gcd(BOXES, 512)

    def aggregate_block(fields):
        return aggregate_boxes(fields, interp_matrix, cosine_part, sine_part)

    def anterpolate_block(fields):
        return anterpolate_boxes(fields, interp_matrix, cosine_part, sine_part)

    def pick_rows(source_rows, order_row):
        return source_rows[order_row]

    def place_rows(values, order_row):
        return jnp.zeros_like(values).at[order_row].set(values)

    blocks = child_fields.reshape(BOXES // block_boxes, block_boxes, CHILDREN, 2, DC)
    parents = lax.map(aggregate_block, blocks).reshape(NPATCH, PB, 2, DP)
    grid = jax.vmap(pick_rows)(parents, patch_order).reshape(NU, PV, 2, DP)

    band_size = 512 if DP % 512 == 0 else DP
    band_count = DP // band_size
    grid_bands = grid.reshape(NU, PV, 2, band_count, band_size).transpose(3, 0, 1, 2, 4)
    ops_bands = operators.reshape(NOPS, 2, band_count, band_size).transpose(2, 0, 1, 3)
    codes = offset_code.transpose(2, 0, 1)
    chosen = operator_index.transpose(2, 0, 1)

    def translate_one(paired):
        return translate_band(paired[0], codes, chosen, paired[1])

    translated = lax.map(translate_one, (grid_bands, ops_bands))
    translated = translated.transpose(1, 2, 3, 0, 4).reshape(NPATCH, PB, 2, DP)
    returned = jax.vmap(place_rows)(translated, patch_order)
    returned = returned.reshape(BOXES // block_boxes, block_boxes, 2, DP)
    local_fields = lax.map(anterpolate_block, returned)
    return local_fields.reshape(BOXES, CHILDREN, 2, DC)
```

```python
import functools

import jax
import jax.numpy as jnp
from jax import lax
from jax.experimental import pallas as pl
from jax.experimental.pallas import tpu as pltpu
from jax.sharding import PartitionSpec as P

BF = jnp.bfloat16
F32 = jnp.float32
I32 = jnp.int32
REACH = 3
SPAN = 2 * REACH + 1


def onehot(mask):
    return jnp.where(mask, jnp.float32(1), jnp.float32(0))


def mm(a, b):
    return jnp.dot(a, b, preferred_element_type=F32)


SIN = (1.0, -0.16666666541438965, 0.008333329264451874, -0.00019840702862140153,
       2.751885561882994e-06, -2.3794713199798423e-08)
COS = (0.4999999954953283, -0.041666640727244325, 0.0013888403499237425,
       -2.476188584583927e-05, 2.6077099012783433e-07)


def horner(coefficients, t):
    value = jnp.full(t.shape, coefficients[-1], F32)
    for c in coefficients[-2::-1]:
        value = value * t + jnp.float32(c)
    return value


def cos_sin(angle):
    half = angle * 0.5
    t = half * half
    sine = half * horner(SIN, t)
    cosine = 1.0 - t * horner(COS, t)
    return (cosine - sine) * (cosine + sine), 2.0 * (sine * cosine)


def grid_of(nd):
    across = nd // 2
    ny = 2 if across % 2 == 0 else 1
    return across // ny, ny


def kernel(
    nd, nb, bc, ch, rows, cols,
    child, interp, phase, order, codes, chosen, ops, out,
    order_v, codes_v, chosen_v, ops_v, child_v, interp_v, phase_v, cos_v, sin_v, send_a, recv_a, cnt, weights, gpad,
    halo_out, halo_in, send_b, recv_b, acc_v,
    load_sem, send_a_sem, recv_a_sem, send_b_sem, recv_b_sem, halo_s_sem, halo_r_sem,
):
    dc, dp = interp.shape
    bw = ops.shape[1]
    nops = ops.shape[0] // 2
    cells = rows * cols
    pair = 2 * bw
    nz, ny = grid_of(nd)
    slots = nz * ny
    me = lax.axis_index("dir")
    mb = lax.axis_index("box")
    up = lax.rem(mb + 1, nb)
    down = lax.rem(mb + nb - 1, nb)
    mx = lax.rem(me, 2)
    mq = lax.div(me, 2)
    my = lax.rem(mq, ny)
    mz = lax.div(mq, ny)

    def hops(offset):
        return sum(min(d, n - d) for d, n in zip(offset, (nz, ny)))

    offsets = sorted(((a, b) for a in range(nz) for b in range(ny)),
                     key=lambda o: (-hops(o), -min(o[0], nz - o[0])))
    ahead = [lax.rem(mz + a, nz) * ny + lax.rem(my + b, ny) for a, b in offsets]
    behind = [lax.rem(mz + nz - a, nz) * ny + lax.rem(my + ny - b, ny) for a, b in offsets]

    loads = [
        pltpu.make_async_copy(child, child_v, load_sem.at[0]),
        pltpu.make_async_copy(phase, phase_v, load_sem.at[1]),
    ]
    for j in range(slots):
        part = pl.ds(pl.multiple_of(ahead[j] * pair, pair), pair)
        loads.append(pltpu.make_async_copy(interp.at[:, part], interp_v.at[j], load_sem.at[2 + j]))
    tables = [
        pltpu.make_async_copy(source, dest, load_sem.at[len(loads) + i])
        for i, (source, dest) in enumerate(
            ((order, order_v), (codes, codes_v), (chosen, chosen_v), (ops, ops_v)))
    ]
    for copy in loads + tables:
        copy.start()

    partners = []
    for j in range(slots):
        for flip in (1, 0):
            if j < slots - 1 or flip:
                partners.append((j, lax.rem(mx + flip, 2), flip))

    barrier = pltpu.get_barrier_semaphore()
    for j, h, flip in partners:
        pl.semaphore_signal(barrier, inc=1, device_id={"dir": ahead[j] * 2 + h},
                            device_id_type=pl.DeviceIdType.MESH)
    edges = (up, down) if nb > 2 else (up,)
    for other in edges:
        pl.semaphore_signal(barrier, inc=1, device_id={"box": other},
                            device_id_type=pl.DeviceIdType.MESH)

    group = 2 * ch
    total = bc * group
    r0 = lax.broadcasted_iota(I32, (total, total), 0)
    r1 = lax.broadcasted_iota(I32, (total, total), 1)
    bshift = bc.bit_length() - 1
    pick = onehot(r1 == (r0 & (bc - 1)) * group + (r0 >> bshift)).astype(BF)
    loads[0].wait()
    x = mm(pick, child_v[...].reshape(total, dc)).astype(BF)
    loads[1].wait()
    for j in range(slots):
        part = pl.ds(pl.multiple_of(ahead[j] * pair, pair), pair)
        cos_v[j], sin_v[j] = cos_sin(phase_v[:, part])

    def combine(j, prod):
        re = jnp.zeros((bc, pair), F32)
        im = jnp.zeros((bc, pair), F32)
        for c in range(ch):
            cc = cos_v[j, c:c + 1]
            ss = sin_v[j, c:c + 1]
            pr = prod[c * 2 * bc:c * 2 * bc + bc]
            pi = prod[c * 2 * bc + bc:(c + 1) * 2 * bc]
            re = re + (cc * pr - ss * pi)
            im = im + (cc * pi + ss * pr)
        block = jnp.concatenate([re, im], axis=0).astype(BF)
        for h in range(2):
            send_a[2 * j + h] = block[:, h * bw:(h + 1) * bw]

    def send_first(j, h):
        return pltpu.make_async_remote_copy(
            src_ref=send_a.at[2 * j + h], dst_ref=recv_a.at[me], send_sem=send_a_sem,
            recv_sem=recv_a_sem, device_id={"dir": ahead[j] * 2 + h},
            device_id_type=pl.DeviceIdType.MESH)

    def send_back(j, h):
        to = behind[j] * 2 + h
        return pltpu.make_async_remote_copy(
            src_ref=send_b.at[to], dst_ref=recv_b.at[2 * j + mx], send_sem=send_b_sem,
            recv_sem=recv_b_sem.at[j], device_id={"dir": to},
            device_id_type=pl.DeviceIdType.MESH)

    def whole(source, dest, s_sem, r_sem, first, count):
        part = pl.ds(first, count)
        return pltpu.make_async_remote_copy(
            src_ref=source.at[part], dst_ref=dest.at[part], send_sem=s_sem, recv_sem=r_sem,
            device_id={"dir": me}, device_id_type=pl.DeviceIdType.MESH)

    last = None
    for j in range(slots):
        loads[2 + j].wait()
        prod = mm(x, interp_v[j])
        if last is not None:
            combine(j - 1, last)
        last = prod
    combine(slots - 1, last)

    pl.semaphore_wait(barrier, nd - 1 + len(edges))
    for j, h, flip in partners:
        send_first(j, h).start()
    recv_a[me] = send_a[2 * (slots - 1) + mx]

    for copy in tables:
        copy.wait()
    q0 = lax.broadcasted_iota(I32, (2 * cells, 2 * cells), 0)
    listed = order_v[...]
    slot = (listed >> bshift) * (2 * bc) + (listed & (bc - 1))
    back = onehot(q0 == jnp.concatenate([slot, slot + bc], axis=1))
    place = jnp.transpose(back).astype(BF)
    back = back.astype(BF)

    o0 = lax.broadcasted_iota(I32, (nops, 2 * nops), 0)
    o1 = lax.broadcasted_iota(I32, (nops, 2 * nops), 1)
    raw = ops_v[...]
    table = jnp.concatenate(
        [mm(onehot(o1 == 2 * o0 + s).astype(BF), raw).astype(BF) for s in range(2)], axis=1)

    half = cells // 2
    nlist = codes.shape[1]
    lanes = ((nlist + 63) // 64) * 64
    fill = jnp.full((half, lanes - nlist), -1, I32)
    code = codes_v[...]
    picked = chosen_v[...]
    both_codes = jnp.concatenate(
        [code[:half], fill, code[half:] + SPAN * SPAN, fill], axis=1)
    both_ops = jnp.concatenate([picked[:half], fill, picked[half:], fill], axis=1)
    span_rows = 2 * SPAN * SPAN
    pad_rows = ((span_rows + 15) // 16) * 16
    m0 = lax.broadcasted_iota(I32, (pad_rows, 2 * lanes), 0)
    n0 = lax.broadcasted_iota(I32, (nops, 2 * lanes), 0)
    for g in range(half):
        left = onehot(m0 == both_codes[g:g + 1]).astype(BF)
        right = onehot(n0 == both_ops[g:g + 1]).astype(BF)
        cnt[g * pad_rows:(g + 1) * pad_rows] = lax.dot_general(
            left, right, (((1,), (1,)), ((), ())), preferred_element_type=F32)
    for f in range(SPAN * SPAN):
        both = jnp.concatenate(
            [cnt[pl.ds(c * SPAN * SPAN + f, half, stride=pad_rows)] for c in range(2)],
            axis=0).astype(BF)
        weight = mm(both, table)
        weights[f, 0] = weight[:, :bw]
        weights[f, 1] = weight[:, bw:]

    whole(send_a, recv_a, send_a_sem, recv_a_sem, 0, nd - 1).wait_recv()
    grid = mm(place, recv_a[...].reshape(2 * cells, bw))
    edge = REACH * cols
    for s in range(2):
        halo_out[0, s] = grid[(s + 1) * cells - edge:(s + 1) * cells].astype(BF)
        halo_out[1, s] = grid[s * cells:s * cells + edge].astype(BF)
    halos = [
        pltpu.make_async_remote_copy(
            src_ref=halo_out.at[w], dst_ref=halo_in.at[w], send_sem=halo_s_sem.at[w],
            recv_sem=halo_r_sem.at[w], device_id={"box": other},
            device_id_type=pl.DeviceIdType.MESH)
        for w, other in ((0, up), (1, down))
    ]
    for copy in halos:
        copy.start()

    def lay(s, first, values):
        count = values.shape[0]
        gpad[s, first:first + count, REACH:REACH + cols] = values
        gpad[s, first:first + count, 0:REACH] = values[:, cols - REACH:]
        gpad[s, first:first + count, REACH + cols:2 * REACH + cols] = values[:, :REACH]

    for s in range(2):
        lay(s, REACH, grid[s * cells:(s + 1) * cells].reshape(rows, cols, bw))

    def gather(source_rows, totals):
        totals = list(totals)
        for dv in range(SPAN):
            for r in source_rows:
                sr = gpad[0, r, dv:dv + cols]
                si = gpad[1, r, dv:dv + cols]
                for u in range(rows):
                    du = r - u
                    if 0 <= du < SPAN:
                        f = du * SPAN + dv
                        wr = weights[f, 0, u * cols:(u + 1) * cols]
                        wi = weights[f, 1, u * cols:(u + 1) * cols]
                        tr, ti = totals[u]
                        totals[u] = (tr + (wr * sr - wi * si), ti + (wr * si + wi * sr))
        return totals

    zero = jnp.zeros((cols, bw), F32)
    totals = gather(range(REACH, REACH + rows), [(zero, zero)] * rows)
    for w, first in ((0, 0), (1, REACH + rows)):
        halos[w].wait_recv()
        for s in range(2):
            lay(s, first, halo_in[w, s].astype(F32).reshape(REACH, cols, bw))
    totals = gather(list(range(REACH)) + list(range(REACH + rows, 2 * REACH + rows)), totals)
    moved = jnp.concatenate(
        [totals[u][s] for s in range(2) for u in range(rows)], axis=0).astype(BF)
    send_b[...] = mm(back, moved).astype(BF).reshape(nd, 2 * bc, bw)
    for j, h, flip in partners:
        send_back(j, h).start()
    recv_b[2 * (slots - 1) + mx] = send_b[me]
    whole(send_a, recv_a, send_a_sem, recv_a_sem, 0, nd - 1).wait_send()
    for copy in halos:
        copy.wait_send()

    def shifted(j):
        block = jnp.concatenate([recv_b[2 * j], recv_b[2 * j + 1]], axis=1).astype(F32)
        re = block[:bc]
        im = block[bc:]
        pieces = []
        for c in range(ch):
            cc = cos_v[j, c:c + 1]
            ss = sin_v[j, c:c + 1]
            pieces.append(cc * re + ss * im)
            pieces.append(cc * im - ss * re)
        return jnp.concatenate(pieces, axis=0).astype(BF)

    near_first = list(range(slots))[::-1]
    for i, j in enumerate(near_first):
        if i == slots - 1:
            whole(send_b, recv_b, send_b_sem, recv_b_sem.at[j], 0, nd - 1).wait_send()
        whole(send_b, recv_b, send_b_sem, recv_b_sem.at[j], 2 * j, 1 if i == 0 else 2).wait_recv()
        term = lax.dot_general(
            shifted(j), interp_v[j], (((1,), (1,)), ((), ())), preferred_element_type=F32)
        if i < slots - 1:
            acc_v[...] = term if i == 0 else acc_v[...] + term
        else:
            out[...] = ((acc_v[...] + term) * (dc / dp)).astype(BF)


def per_device(nd, nb, child, interp, phase, order, codes, chosen, operators):
    bc, ch, _, dc = child.shape
    dp = interp.shape[1]
    rows, cols, nlist = codes.shape
    nops, _, bw = operators.shape
    cells = rows * cols
    nz, ny = grid_of(nd)
    slots = nz * ny
    lanes = ((nlist + 63) // 64) * 64
    pad_rows = ((2 * SPAN * SPAN + 15) // 16) * 16
    total = bc * ch * 2
    vmem = pl.BlockSpec(memory_space=pltpu.VMEM)
    hbm = pl.BlockSpec(memory_space=pltpu.HBM)
    result = pl.pallas_call(
        functools.partial(kernel, nd, nb, bc, ch, rows, cols),
        out_shape=jax.ShapeDtypeStruct((total, dc), BF),
        in_specs=[hbm] * 7,
        out_specs=vmem,
        scratch_shapes=[
            pltpu.VMEM(order.shape, I32),
            pltpu.VMEM((cells, nlist), I32),
            pltpu.VMEM((cells, nlist), I32),
            pltpu.VMEM((nops * 2, bw), BF),
            pltpu.VMEM((bc * ch, 2, dc), BF),
            pltpu.VMEM((slots, dc, 2 * bw), BF),
            pltpu.VMEM((ch, dp), F32),
            pltpu.VMEM((slots, ch, 2 * bw), F32),
            pltpu.VMEM((slots, ch, 2 * bw), F32),
            pltpu.VMEM((nd, 2 * bc, bw), BF),
            pltpu.VMEM((nd, 2 * bc, bw), BF),
            pltpu.VMEM((cells // 2 * pad_rows, nops), F32),
            pltpu.VMEM((SPAN * SPAN, 2, cells, bw), F32),
            pltpu.VMEM((2, rows + 2 * REACH, 24, bw), F32),
            pltpu.VMEM((2, 2, REACH * cols, bw), BF),
            pltpu.VMEM((2, 2, REACH * cols, bw), BF),
            pltpu.VMEM((nd, 2 * bc, bw), BF),
            pltpu.VMEM((nd, 2 * bc, bw), BF),
            pltpu.VMEM((total, dc), F32),
            pltpu.SemaphoreType.DMA((6 + slots,)),
            pltpu.SemaphoreType.DMA,
            pltpu.SemaphoreType.DMA,
            pltpu.SemaphoreType.DMA,
            pltpu.SemaphoreType.DMA((slots,)),
            pltpu.SemaphoreType.DMA((2,)),
            pltpu.SemaphoreType.DMA((2,)),
        ],
        compiler_params=pltpu.CompilerParams(
            collective_id=0, has_side_effects=True, vmem_limit_bytes=24 * 2 ** 20),
    )(*(
        pltpu.with_memory_space_constraint(value, pltpu.HBM)
        for value in (
            child.reshape(bc * ch, 2, dc), interp, phase, order,
            codes.reshape(cells, nlist), chosen.reshape(cells, nlist),
            operators.reshape(nops * 2, bw),
        )
    ))
    return result.reshape(ch, 2, bc, dc).transpose(2, 0, 1, 3)


def solution(mesh):
    in_specs = (
        P(("box", "dir"), None, None, None),
        P(),
        P(),
        P("box", None),
        P("box", None, None),
        P("box", None, None),
        P(None, None, "dir"),
    )
    out_specs = P(("box", "dir"), None, None, None)
    return jax.shard_map(
        functools.partial(per_device, mesh.shape["dir"], mesh.shape["box"]),
        mesh=mesh, in_specs=in_specs, out_specs=out_specs, check_vma=False,
    )
```

```python
import functools

import jax
import jax.numpy as jnp
from jax import lax
from jax.experimental import pallas as pl
from jax.experimental.pallas import tpu as pltpu
from jax.sharding import PartitionSpec as P

BF = jnp.bfloat16
F32 = jnp.float32
I32 = jnp.int32
REACH = 3
SPAN = 2 * REACH + 1


def onehot(mask):
    return jnp.where(mask, jnp.float32(1), jnp.float32(0))


def mm(a, b):
    return jnp.dot(a, b, preferred_element_type=F32)


SIN = (1.0, -0.16666666541438965, 0.008333329264451874, -0.00019840702862140153,
       2.751885561882994e-06, -2.3794713199798423e-08)
COS = (0.4999999954953283, -0.041666640727244325, 0.0013888403499237425,
       -2.476188584583927e-05, 2.6077099012783433e-07)


def horner(coefficients, t):
    value = jnp.full(t.shape, coefficients[-1], F32)
    for c in coefficients[-2::-1]:
        value = value * t + jnp.float32(c)
    return value


def cos_sin(angle):
    half = angle * 0.5
    t = half * half
    sine = half * horner(SIN, t)
    cosine = 1.0 - t * horner(COS, t)
    return (cosine - sine) * (cosine + sine), 2.0 * (sine * cosine)


def grid_of(nd):
    across = nd // 2
    ny = 2 if across % 2 == 0 else 1
    return across // ny, ny


def kernel(
    nd, nb, bc, ch, rows, cols,
    child, interp, phase, order, codes, chosen, ops, out,
    order_v, codes_v, chosen_v, ops_v, child_v, interp_v, phase_v, cos_v, sin_v, send_a, recv_a, cnt, weights, gpad,
    halo_out, halo_in, send_b, recv_b, acc_v, interp_t,
    slot_sem, recv_a_sem, halo_s_sem, halo_r_sem, child_sem, phase_sem, order_sem, codes_sem, ops_sem,
):
    dc, dp = interp.shape
    bw = ops.shape[1]
    nops = ops.shape[0] // 2
    cells = rows * cols
    pair = 2 * bw
    nz, ny = grid_of(nd)
    slots = nz * ny
    me = lax.axis_index("dir")
    mb = lax.axis_index("box")
    up = lax.rem(mb + 1, nb)
    down = lax.rem(mb + nb - 1, nb)
    mx = lax.rem(me, 2)
    mq = lax.div(me, 2)
    my = lax.rem(mq, ny)
    mz = lax.div(mq, ny)

    def hops(offset):
        return sum(min(d, n - d) for d, n in zip(offset, (nz, ny)))

    offsets = [(a, b) for a in range(nz) for b in range(ny)]
    far = sorted(range(slots), key=lambda j: (-hops(offsets[j]), -min(offsets[j][0], nz - offsets[j][0])))

    def slot_of(a, b):
        return a * ny + b

    def reach(d):
        return d // 2 // ny + d // 2 % ny + d % 2

    ahead = [lax.rem(mz + a, nz) * ny + lax.rem(my + b, ny) for a, b in offsets]
    behind = [lax.rem(mz + nz - a, nz) * ny + lax.rem(my + ny - b, ny) for a, b in offsets]

    partners = []
    for j in far:
        for flip in (1, 0):
            if j or flip:
                partners.append((j, lax.rem(mx + flip, 2), flip))

    barrier = pltpu.get_barrier_semaphore()
    for j, h, flip in partners:
        pl.semaphore_signal(barrier, inc=1, device_id={"dir": ahead[j] * 2 + h},
                            device_id_type=pl.DeviceIdType.MESH)
    edges = (up, down) if nb > 2 else (up,)
    for other in edges:
        pl.semaphore_signal(barrier, inc=1, device_id={"box": other},
                            device_id_type=pl.DeviceIdType.MESH)

    first_loads = [
        pltpu.make_async_copy(child, child_v, child_sem),
        pltpu.make_async_copy(phase, phase_v, phase_sem),
    ]
    columns = []
    for i, j in enumerate(far):
        part = pl.ds(pl.multiple_of(ahead[j] * pair, pair), pair)
        columns.append(pltpu.make_async_copy(interp.at[:, part], interp_v.at[j], slot_sem.at[i]))
    tables = [
        pltpu.make_async_copy(source, dest, sem)
        for source, dest, sem in (
            (order, order_v, order_sem), (codes, codes_v, codes_sem), (chosen, chosen_v, halo_s_sem), (ops, ops_v, ops_sem))
    ]
    for copy in first_loads + columns + tables:
        copy.start()

    group = 2 * ch
    total = bc * group
    r0 = lax.broadcasted_iota(I32, (total, total), 0)
    r1 = lax.broadcasted_iota(I32, (total, total), 1)
    bshift = bc.bit_length() - 1
    pick = onehot(r1 == (r0 & (bc - 1)) * group + (r0 >> bshift)).astype(BF)
    first_loads[0].wait()
    x = mm(pick, child_v[...].reshape(total, dc)).astype(BF)
    first_loads[1].wait()
    for j in range(slots):
        part = pl.ds(pl.multiple_of(ahead[j] * pair, pair), pair)
        cos_v[j], sin_v[j] = cos_sin(phase_v[:, part])

    def combine(j, prod):
        re = jnp.zeros((bc, pair), F32)
        im = jnp.zeros((bc, pair), F32)
        for c in range(ch):
            cc = cos_v[j, c:c + 1]
            ss = sin_v[j, c:c + 1]
            pr = prod[c * 2 * bc:c * 2 * bc + bc]
            pi = prod[c * 2 * bc + bc:(c + 1) * 2 * bc]
            re = re + (cc * pr - ss * pi)
            im = im + (cc * pi + ss * pr)
        block = jnp.concatenate([re, im], axis=0).astype(BF)
        for h in range(2):
            send_a[2 * j + h] = block[:, h * bw:(h + 1) * bw]

    def send_first(j, h):
        return pltpu.make_async_remote_copy(
            src_ref=send_a.at[2 * j + h], dst_ref=recv_a.at[me], send_sem=child_sem,
            recv_sem=recv_a_sem, device_id={"dir": ahead[j] * 2 + h},
            device_id_type=pl.DeviceIdType.MESH)

    def send_back(j, h):
        to = behind[j] * 2 + h
        return pltpu.make_async_remote_copy(
            src_ref=send_b.at[to], dst_ref=recv_b.at[2 * j + mx], send_sem=phase_sem,
            recv_sem=slot_sem.at[j], device_id={"dir": to},
            device_id_type=pl.DeviceIdType.MESH)

    def whole(source, dest, s_sem, r_sem, first, count):
        part = pl.ds(first, count)
        return pltpu.make_async_remote_copy(
            src_ref=source.at[part], dst_ref=dest.at[part], send_sem=s_sem, recv_sem=r_sem,
            device_id={"dir": me}, device_id_type=pl.DeviceIdType.MESH)

    last = None
    for i, j in enumerate(far):
        columns[i].wait()
        prod = mm(x, interp_v[j])
        if last is not None:
            combine(far[i - 1], last)
        last = prod
    combine(0, last)

    pl.semaphore_wait(barrier, nd - 1 + len(edges))
    for to in sorted(range(nd), key=lambda d: (-reach(d), -d)):
        @pl.when(me != to)
        def _():
            a, b = to // 2 // ny, to // 2 % ny
            place = slot_of(lax.rem(a + nz - mz, nz), lax.rem(b + ny - my, ny))
            pltpu.make_async_remote_copy(
                src_ref=send_a.at[2 * place + to % 2], dst_ref=recv_a.at[me], send_sem=child_sem,
                recv_sem=recv_a_sem, device_id={"dir": to},
                device_id_type=pl.DeviceIdType.MESH).start()
    recv_a[me] = send_a[mx]

    for copy in tables:
        copy.wait()

    q0 = lax.broadcasted_iota(I32, (2 * cells, 2 * cells), 0)
    listed = order_v[...]
    slot = (listed >> bshift) * (2 * bc) + (listed & (bc - 1))
    back = onehot(q0 == jnp.concatenate([slot, slot + bc], axis=1))
    place = jnp.transpose(back).astype(BF)
    back = back.astype(BF)

    o0 = lax.broadcasted_iota(I32, (nops, 2 * nops), 0)
    o1 = lax.broadcasted_iota(I32, (nops, 2 * nops), 1)
    raw = ops_v[...]
    table = jnp.concatenate(
        [mm(onehot(o1 == 2 * o0 + s).astype(BF), raw).astype(BF) for s in range(2)], axis=1)

    half = cells // 2
    nlist = codes.shape[1]
    lanes = ((nlist + 63) // 64) * 64
    fill = jnp.full((half, lanes - nlist), -1, I32)
    code = codes_v[...]
    picked = chosen_v[...]
    both_codes = jnp.concatenate(
        [code[:half], fill, code[half:] + SPAN * SPAN, fill], axis=1)
    both_ops = jnp.concatenate([picked[:half], fill, picked[half:], fill], axis=1)
    span_rows = 2 * SPAN * SPAN
    pad_rows = ((span_rows + 15) // 16) * 16
    m0 = lax.broadcasted_iota(I32, (pad_rows, 2 * lanes), 0)
    n0 = lax.broadcasted_iota(I32, (nops, 2 * lanes), 0)
    for g in range(half):
        left = onehot(m0 == both_codes[g:g + 1]).astype(BF)
        right = onehot(n0 == both_ops[g:g + 1]).astype(BF)
        cnt[g * pad_rows:(g + 1) * pad_rows] = lax.dot_general(
            left, right, (((1,), (1,)), ((), ())), preferred_element_type=F32)
    for f in range(SPAN * SPAN):
        both = jnp.concatenate(
            [cnt[pl.ds(c * SPAN * SPAN + f, half, stride=pad_rows)] for c in range(2)],
            axis=0).astype(BF)
        weight = mm(both, table)
        wr, wi = weight[:, :bw], weight[:, bw:]
        weights[f, 0] = wr
        weights[f, 1] = wr + wi
        weights[f, 2] = wi - wr

    whole(send_a, recv_a, child_sem, recv_a_sem, 0, nd - 1).wait_recv()
    grid = mm(place, recv_a[...].reshape(2 * cells, bw))
    edge = REACH * cols
    for s in range(2):
        halo_out[0, s] = grid[(s + 1) * cells - edge:(s + 1) * cells].astype(BF)
        halo_out[1, s] = grid[s * cells:s * cells + edge].astype(BF)
    halos = [
        pltpu.make_async_remote_copy(
            src_ref=halo_out.at[w], dst_ref=halo_in.at[w], send_sem=halo_s_sem,
            recv_sem=halo_r_sem, device_id={"box": other},
            device_id_type=pl.DeviceIdType.MESH)
        for w, other in ((0, up), (1, down))
    ]
    for copy in halos:
        copy.start()

    def lay(first, re, im):
        count = re.shape[0]
        for s, values in enumerate((re + im, im, re)):
            gpad[s, first:first + count, REACH:REACH + cols] = values
            gpad[s, first:first + count, 0:REACH] = values[:, cols - REACH:]
            gpad[s, first:first + count, REACH + cols:2 * REACH + cols] = values[:, :REACH]

    lay(REACH, *(grid[s * cells:(s + 1) * cells].reshape(rows, cols, bw) for s in range(2)))

    tile = 8
    def gather(source_rows, totals):
        totals = dict(totals)
        for v in range(0, cols, tile):
            for dv in range(SPAN):
                for r in source_rows:
                    source = [gpad[s, r, v + dv:v + dv + tile] for s in range(3)]
                    for u in range(rows):
                        du = r - u
                        if 0 <= du < SPAN:
                            f = du * SPAN + dv
                            at = slice(u * cols + v, u * cols + v + tile)
                            totals[u, v] = [
                                t + weights[f, s, at] * source[s] for s, t in enumerate(totals[u, v])]
        return totals

    zero = jnp.zeros((tile, bw), F32)
    totals = {(u, v): [zero] * 3 for u in range(rows) for v in range(0, cols, tile)}
    totals = gather(range(REACH, REACH + rows), totals)
    both_halos = pltpu.make_async_remote_copy(
        src_ref=halo_out, dst_ref=halo_in, send_sem=halo_s_sem, recv_sem=halo_r_sem,
        device_id={"box": mb}, device_id_type=pl.DeviceIdType.MESH)
    both_halos.wait_recv()
    for w, first in ((0, 0), (1, REACH + rows)):
        lay(first, *(halo_in[w, s].astype(F32).reshape(REACH, cols, bw) for s in range(2)))
    totals = gather(list(range(REACH)) + list(range(REACH + rows, 2 * REACH + rows)), totals)
    moved = jnp.concatenate([k[0] - k[1] for k in totals.values()] + [k[0] + k[2] for k in totals.values()], axis=0).astype(BF)
    send_b[...] = mm(back, moved).astype(BF).reshape(nd, 2 * bc, bw)
    for to in sorted(range(nd), key=lambda d: (reach(d), d)):
        @pl.when(me != to)
        def _():
            a, b = to // 2 // ny, to // 2 % ny
            place = slot_of(lax.rem(mz + nz - a, nz), lax.rem(my + ny - b, ny))
            pltpu.make_async_remote_copy(
                src_ref=send_b.at[to], dst_ref=recv_b.at[2 * place + mx], send_sem=phase_sem,
                recv_sem=slot_sem.at[place], device_id={"dir": to},
                device_id_type=pl.DeviceIdType.MESH).start()
    recv_b[mx] = send_b[me]
    whole(send_a, recv_a, child_sem, recv_a_sem, 0, nd - 1).wait_send()
    both_halos.wait_send()

    for j in range(slots):
        interp_t[j] = jnp.transpose(interp_v[j])

    def shifted(j):
        block = jnp.concatenate([recv_b[2 * j], recv_b[2 * j + 1]], axis=1).astype(F32)
        re = block[:bc]
        im = block[bc:]
        pieces = []
        for c in range(ch):
            cc = cos_v[j, c:c + 1]
            ss = sin_v[j, c:c + 1]
            pieces.append(cc * re + ss * im)
            pieces.append(cc * im - ss * re)
        return jnp.concatenate(pieces, axis=0).astype(BF)

    near_first = far[::-1]
    for i, j in enumerate(near_first):
        if i == slots - 1:
            whole(send_b, recv_b, phase_sem, slot_sem.at[j], 0, nd - 1).wait_send()
        whole(send_b, recv_b, phase_sem, slot_sem.at[j], 2 * j, 1 if i == 0 else 2).wait_recv()
        term = mm(shifted(j), interp_t[j])
        if i < slots - 1:
            acc_v[...] = term if i == 0 else acc_v[...] + term
        else:
            out[...] = ((acc_v[...] + term) * (dc / dp)).astype(BF)


def per_device(nd, nb, child, interp, phase, order, codes, chosen, operators):
    bc, ch, _, dc = child.shape
    dp = interp.shape[1]
    rows, cols, nlist = codes.shape
    nops, _, bw = operators.shape
    cells = rows * cols
    nz, ny = grid_of(nd)
    slots = nz * ny
    lanes = ((nlist + 63) // 64) * 64
    pad_rows = ((2 * SPAN * SPAN + 15) // 16) * 16
    total = bc * ch * 2
    vmem = pl.BlockSpec(memory_space=pltpu.VMEM)
    hbm = pl.BlockSpec(memory_space=pltpu.HBM)
    result = pl.pallas_call(
        functools.partial(kernel, nd, nb, bc, ch, rows, cols),
        out_shape=jax.ShapeDtypeStruct((total, dc), BF),
        in_specs=[hbm] * 7,
        out_specs=vmem,
        scratch_shapes=[
            pltpu.VMEM(order.shape, I32),
            pltpu.VMEM((cells, nlist), I32),
            pltpu.VMEM((cells, nlist), I32),
            pltpu.VMEM((nops * 2, bw), BF),
            pltpu.VMEM((bc * ch, 2, dc), BF),
            pltpu.VMEM((slots, dc, 2 * bw), BF),
            pltpu.VMEM((ch, dp), F32),
            pltpu.VMEM((slots, ch, 2 * bw), F32),
            pltpu.VMEM((slots, ch, 2 * bw), F32),
            pltpu.VMEM((nd, 2 * bc, bw), BF),
            pltpu.VMEM((nd, 2 * bc, bw), BF),
            pltpu.VMEM((cells // 2 * pad_rows, nops), F32),
            pltpu.VMEM((SPAN * SPAN, 3, cells, bw), F32),
            pltpu.VMEM((3, rows + 2 * REACH, 24, bw), F32),
            pltpu.VMEM((2, 2, REACH * cols, bw), BF),
            pltpu.VMEM((2, 2, REACH * cols, bw), BF),
            pltpu.VMEM((nd, 2 * bc, bw), BF),
            pltpu.VMEM((nd, 2 * bc, bw), BF),
            pltpu.VMEM((total, dc), F32),
            pltpu.VMEM((slots, 2 * bw, dc), BF),
            pltpu.SemaphoreType.DMA((slots,)),
            pltpu.SemaphoreType.DMA,
            pltpu.SemaphoreType.DMA,
            pltpu.SemaphoreType.DMA,
            pltpu.SemaphoreType.DMA,
            pltpu.SemaphoreType.DMA,
            pltpu.SemaphoreType.DMA,
            pltpu.SemaphoreType.DMA,
            pltpu.SemaphoreType.DMA,
        ],
        compiler_params=pltpu.CompilerParams(
            collective_id=0, has_side_effects=True, vmem_limit_bytes=32 * 2 ** 20),
    )(*(
        pltpu.with_memory_space_constraint(value, pltpu.HBM)
        for value in (
            child.reshape(bc * ch, 2, dc), interp, phase, order,
            codes.reshape(cells, nlist), chosen.reshape(cells, nlist),
            operators.reshape(nops * 2, bw),
        )
    ))
    return result.reshape(ch, 2, bc, dc).transpose(2, 0, 1, 3)


def solution(mesh):
    in_specs = (
        P(("box", "dir"), None, None, None),
        P(),
        P(),
        P("box", None),
        P("box", None, None),
        P("box", None, None),
        P(None, None, "dir"),
    )
    out_specs = P(("box", "dir"), None, None, None)
    return jax.shard_map(
        functools.partial(per_device, mesh.shape["dir"], mesh.shape["box"]),
        mesh=mesh, in_specs=in_specs, out_specs=out_specs, check_vma=False,
    )
```

```python
import functools

import jax
import jax.numpy as jnp
from jax import lax
from jax.experimental import pallas as pl
from jax.experimental.pallas import tpu as pltpu
from jax.sharding import PartitionSpec as P

BF = jnp.bfloat16
F32 = jnp.float32
I32 = jnp.int32
REACH = 3
SPAN = 2 * REACH + 1


def onehot(mask):
    return jnp.where(mask, jnp.float32(1), jnp.float32(0))


def mm(a, b):
    return jnp.dot(a, b, preferred_element_type=F32)


SIN = (1.0, -0.16666666541438965, 0.008333329264451874, -0.00019840702862140153,
       2.751885561882994e-06, -2.3794713199798423e-08)
COS = (0.4999999954953283, -0.041666640727244325, 0.0013888403499237425,
       -2.476188584583927e-05, 2.6077099012783433e-07)


def horner(coefficients, t):
    value = jnp.full(t.shape, coefficients[-1], F32)
    for c in coefficients[-2::-1]:
        value = value * t + jnp.float32(c)
    return value


def cos_sin(angle):
    half = angle * 0.5
    t = half * half
    sine = half * horner(SIN, t)
    cosine = 1.0 - t * horner(COS, t)
    return (cosine - sine) * (cosine + sine), 2.0 * (sine * cosine)


def grid_of(nd):
    across = nd // 2
    ny = 2 if across % 2 == 0 else 1
    return across // ny, ny


def kernel(
    nd, nb, bc, ch, rows, cols,
    child, interp, phase, order, codes, chosen, ops, out,
    order_v, codes_v, chosen_v, ops_v, child_v, interp_v, phase_v, cos_v, sin_v, send_a, recv_a, cnt, weights, gpad,
    halo_out, halo_in, send_b, recv_b, acc_v, interp_t, first_w, first_in, first_halo, send_first_b,
    slot_sem, recv_a_sem, halo_s_sem, halo_r_sem, child_sem, phase_sem, order_sem, codes_sem, ops_sem,
):
    dc, dp = interp.shape
    bw = ops.shape[1]
    nops = ops.shape[0] // 2
    cells = rows * cols
    pair = 2 * bw
    nz, ny = grid_of(nd)
    slots = nz * ny
    me = lax.axis_index("dir")
    mb = lax.axis_index("box")
    up = lax.rem(mb + 1, nb)
    down = lax.rem(mb + nb - 1, nb)
    mx = lax.rem(me, 2)
    mq = lax.div(me, 2)
    my = lax.rem(mq, ny)
    mz = lax.div(mq, ny)

    def hops(offset):
        return sum(min(d, n - d) for d, n in zip(offset, (nz, ny)))

    offsets = [(a, b) for a in range(nz) for b in range(ny)]
    far = sorted(range(slots), key=lambda j: (-hops(offsets[j]), -min(offsets[j][0], nz - offsets[j][0])))

    def slot_of(a, b):
        return a * ny + b

    def reach(d):
        return d // 2 // ny + d // 2 % ny + d % 2

    ahead = [lax.rem(mz + a, nz) * ny + lax.rem(my + b, ny) for a, b in offsets]
    behind = [lax.rem(mz + nz - a, nz) * ny + lax.rem(my + ny - b, ny) for a, b in offsets]

    partners = []
    for j in far:
        for flip in (1, 0):
            if j or flip:
                partners.append((j, lax.rem(mx + flip, 2), flip))

    barrier = pltpu.get_barrier_semaphore()
    for j, h, flip in partners:
        pl.semaphore_signal(barrier, inc=1, device_id={"dir": ahead[j] * 2 + h},
                            device_id_type=pl.DeviceIdType.MESH)
    edges = (up, down) if nb > 2 else (up,)
    for other in edges:
        pl.semaphore_signal(barrier, inc=1, device_id={"box": other},
                            device_id_type=pl.DeviceIdType.MESH)

    first_loads = [
        pltpu.make_async_copy(child, child_v, child_sem),
        pltpu.make_async_copy(phase, phase_v, phase_sem),
    ]
    columns = []
    for i, j in enumerate(far):
        part = pl.ds(pl.multiple_of(ahead[j] * pair, pair), pair)
        columns.append(pltpu.make_async_copy(interp.at[:, part], interp_v.at[j], slot_sem.at[i]))
    tables = [
        pltpu.make_async_copy(source, dest, sem)
        for source, dest, sem in (
            (order, order_v, order_sem), (codes, codes_v, codes_sem), (chosen, chosen_v, halo_s_sem), (ops, ops_v, ops_sem))
    ]
    for copy in first_loads + columns + tables:
        copy.start()

    group = 2 * ch
    total = bc * group
    r0 = lax.broadcasted_iota(I32, (total, total), 0)
    r1 = lax.broadcasted_iota(I32, (total, total), 1)
    bshift = bc.bit_length() - 1
    pick = onehot(r1 == (r0 & (bc - 1)) * group + (r0 >> bshift)).astype(BF)
    first_loads[0].wait()
    x = mm(pick, child_v[...].reshape(total, dc)).astype(BF)
    first_loads[1].wait()
    for j in range(slots):
        part = pl.ds(pl.multiple_of(ahead[j] * pair, pair), pair)
        cos_v[j], sin_v[j] = cos_sin(phase_v[:, part])

    def combine(j, prod):
        re = jnp.zeros((bc, pair), F32)
        im = jnp.zeros((bc, pair), F32)
        for c in range(ch):
            cc = cos_v[j, c:c + 1]
            ss = sin_v[j, c:c + 1]
            pr = prod[c * 2 * bc:c * 2 * bc + bc]
            pi = prod[c * 2 * bc + bc:(c + 1) * 2 * bc]
            re = re + (cc * pr - ss * pi)
            im = im + (cc * pi + ss * pr)
        block = jnp.concatenate([re, im], axis=0).astype(BF)
        for h in range(2):
            send_a[2 * j + h] = block[:, h * bw:(h + 1) * bw]

    def send_first(j, h):
        return pltpu.make_async_remote_copy(
            src_ref=send_a.at[2 * j + h], dst_ref=recv_a.at[me], send_sem=child_sem,
            recv_sem=recv_a_sem, device_id={"dir": ahead[j] * 2 + h},
            device_id_type=pl.DeviceIdType.MESH)

    def send_back(j, h):
        to = behind[j] * 2 + h
        return pltpu.make_async_remote_copy(
            src_ref=send_b.at[to], dst_ref=recv_b.at[2 * j + mx], send_sem=phase_sem,
            recv_sem=slot_sem.at[j], device_id={"dir": to},
            device_id_type=pl.DeviceIdType.MESH)

    def whole(source, dest, s_sem, r_sem, first, count):
        part = pl.ds(first, count)
        return pltpu.make_async_remote_copy(
            src_ref=source.at[part], dst_ref=dest.at[part], send_sem=s_sem, recv_sem=r_sem,
            device_id={"dir": me}, device_id_type=pl.DeviceIdType.MESH)

    last = None
    for i, j in enumerate(far):
        columns[i].wait()
        prod = mm(x, interp_v[j])
        if last is not None:
            combine(far[i - 1], last)
        last = prod
    combine(0, last)

    pl.semaphore_wait(barrier, nd - 1 + len(edges))
    for to in sorted(range(nd), key=lambda d: (-reach(d), -d)):
        @pl.when(me != to)
        def _():
            a, b = to // 2 // ny, to // 2 % ny
            place = slot_of(lax.rem(a + nz - mz, nz), lax.rem(b + ny - my, ny))
            pltpu.make_async_remote_copy(
                src_ref=send_a.at[2 * place + to % 2], dst_ref=recv_a.at[me], send_sem=child_sem,
                recv_sem=recv_a_sem, device_id={"dir": to},
                device_id_type=pl.DeviceIdType.MESH).start()
    recv_a[me] = send_a[mx]

    for copy in tables:
        copy.wait()

    q0 = lax.broadcasted_iota(I32, (2 * cells, 2 * cells), 0)
    listed = order_v[...]
    slot = (listed >> bshift) * (2 * bc) + (listed & (bc - 1))
    back = onehot(q0 == jnp.concatenate([slot, slot + bc], axis=1))
    place = jnp.transpose(back).astype(BF)
    back = back.astype(BF)

    o0 = lax.broadcasted_iota(I32, (nops, 2 * nops), 0)
    o1 = lax.broadcasted_iota(I32, (nops, 2 * nops), 1)
    raw = ops_v[...]
    table = jnp.concatenate(
        [mm(onehot(o1 == 2 * o0 + s).astype(BF), raw).astype(BF) for s in range(2)], axis=1)

    half = cells // 2
    nlist = codes.shape[1]
    lanes = ((nlist + 63) // 64) * 64
    fill = jnp.full((half, lanes - nlist), -1, I32)
    code = codes_v[...]
    picked = chosen_v[...]
    both_codes = jnp.concatenate(
        [code[:half], fill, code[half:] + SPAN * SPAN, fill], axis=1)
    both_ops = jnp.concatenate([picked[:half], fill, picked[half:], fill], axis=1)
    span_rows = 2 * SPAN * SPAN
    pad_rows = ((span_rows + 15) // 16) * 16
    m0 = lax.broadcasted_iota(I32, (pad_rows, 2 * lanes), 0)
    n0 = lax.broadcasted_iota(I32, (nops, 2 * lanes), 0)
    for g in range(half):
        left = onehot(m0 == both_codes[g:g + 1]).astype(BF)
        right = onehot(n0 == both_ops[g:g + 1]).astype(BF)
        cnt[g * pad_rows:(g + 1) * pad_rows] = lax.dot_general(
            left, right, (((1,), (1,)), ((), ())), preferred_element_type=F32)
    for f in range(SPAN * SPAN):
        both = jnp.concatenate(
            [cnt[pl.ds(c * SPAN * SPAN + f, half, stride=pad_rows)] for c in range(2)],
            axis=0).astype(BF)
        weight = mm(both, table)
        wr, wi = weight[:, :bw], weight[:, bw:]
        weights[f, 0] = wr
        weights[f, 1] = wr + wi
        weights[f, 2] = wi - wr

    edge = REACH * cols
    spans = SPAN * SPAN
    entries = spans + spans % 2

    def prepare_first():
        cshift = cols.bit_length() - 1
        held = onehot(listed == lax.broadcasted_iota(I32, (bc, cells), 0))
        cell = lax.broadcasted_iota(I32, (bc, cells), 1)
        home_u = jnp.sum(held * (cell >> cshift).astype(F32), axis=1, keepdims=True).astype(I32)
        home_v = jnp.sum(held * (cell & (cols - 1)).astype(F32), axis=1, keepdims=True).astype(I32)
        held = held.astype(BF)
        none = jnp.full((bc, lanes - nlist), -1, I32)
        own_code = jnp.concatenate([mm(held, code.astype(F32).astype(BF)).astype(I32), none], axis=1)
        own_ops = jnp.concatenate([mm(held, picked.astype(F32).astype(BF)).astype(I32), none], axis=1)
        box_rows = ((spans + 15) // 16) * 16
        m1 = lax.broadcasted_iota(I32, (box_rows, lanes), 0)
        n1 = lax.broadcasted_iota(I32, (nops, lanes), 0)
        for g in range(bc):
            left = onehot(m1 == own_code[g:g + 1]).astype(BF)
            right = onehot(n1 == own_ops[g:g + 1]).astype(BF)
            cnt[g * box_rows:(g + 1) * box_rows] = lax.dot_general(
                left, right, (((1,), (1,)), ((), ())), preferred_element_type=F32)
        times = [cnt[pl.ds(f, bc, stride=box_rows)] for f in range(spans)]
        times += [jnp.zeros((bc, nops), F32)] * (entries - spans)
        weight = mm(jnp.concatenate(times, axis=0).astype(BF), table)
        wr, wi = weight[:, :bw], weight[:, bw:]
        first_w[0] = wr
        first_w[1] = wr + wi
        first_w[2] = wi - wr

        lane = lax.broadcasted_iota(I32, (bc, cells), 1)
        halo_lane = lax.broadcasted_iota(I32, (bc, 4 * edge), 1)
        wide_u = jnp.broadcast_to(home_u, (bc, 4 * edge))
        wide_v = jnp.broadcast_to(home_v, (bc, 4 * edge))
        inside, beyond = [], [[], []]
        for f in range(entries):
            r = wide_u + (f // SPAN - REACH)
            at = r * cols + ((wide_v + (f % SPAN - REACH)) & (cols - 1))
            inside.append(onehot(at[:, :cells] == lane))
            past = jnp.where(r < 0, at + edge, jnp.where(r >= rows, at - cells + 2 * edge, -4 * edge))
            for s in range(2):
                beyond[s].append(onehot(past + s * edge == halo_lane))
        inside = jnp.concatenate(inside, axis=0).astype(BF)
        for s in range(2):
            part = slice(s * entries * bc, (s + 1) * entries * bc)
            first_in[part] = mm(inside, place[s * cells:(s + 1) * cells]).astype(BF)
            first_halo[part] = jnp.concatenate(beyond[s], axis=0).astype(BF)

    late_core = lax.rem(mb, 2)
    pl.when(late_core == 0)(prepare_first)

    whole(send_a, recv_a, child_sem, recv_a_sem, 0, nd - 1).wait_recv()
    grid = mm(place, recv_a[...].reshape(2 * cells, bw))
    for s in range(2):
        halo_out[0, s] = grid[(s + 1) * cells - edge:(s + 1) * cells].astype(BF)
        halo_out[1, s] = grid[s * cells:s * cells + edge].astype(BF)
    halos = [
        pltpu.make_async_remote_copy(
            src_ref=halo_out.at[w], dst_ref=halo_in.at[w], send_sem=halo_s_sem,
            recv_sem=halo_r_sem, device_id={"box": other},
            device_id_type=pl.DeviceIdType.MESH)
        for w, other in ((0, up), (1, down))
    ]
    for copy in halos:
        copy.start()
    pl.when(late_core != 0)(prepare_first)
    both_halos = pltpu.make_async_remote_copy(
        src_ref=halo_out, dst_ref=halo_in, send_sem=halo_s_sem, recv_sem=halo_r_sem,
        device_id={"box": mb}, device_id_type=pl.DeviceIdType.MESH)

    @pl.when(me != 0)
    def _():
        both_halos.wait_recv()
        found = mm(first_in[...], recv_a[...].reshape(2 * cells, bw)) + mm(
            first_halo[...], halo_in[...].reshape(4 * edge, bw))
        sums = [jnp.zeros((bc, bw), F32)] * 3
        for f in range(spans):
            re = found[f * bc:(f + 1) * bc]
            im = found[(entries + f) * bc:(entries + f + 1) * bc]
            sums = [t + first_w[s, f * bc:(f + 1) * bc] * z for s, (t, z) in enumerate(zip(sums, (re + im, im, re)))]
        send_first_b[...] = jnp.concatenate([sums[0] - sums[1], sums[0] + sums[2]], axis=0).astype(BF)
        slot = slot_of(mz, my)
        pltpu.make_async_remote_copy(
            src_ref=send_first_b, dst_ref=recv_b.at[2 * slot + mx], send_sem=phase_sem,
            recv_sem=slot_sem.at[slot], device_id={"dir": 0},
            device_id_type=pl.DeviceIdType.MESH).start()

    def lay(first, re, im):
        count = re.shape[0]
        for s, values in enumerate((re + im, im, re)):
            gpad[s, first:first + count, REACH:REACH + cols] = values
            gpad[s, first:first + count, 0:REACH] = values[:, cols - REACH:]
            gpad[s, first:first + count, REACH + cols:2 * REACH + cols] = values[:, :REACH]

    lay(REACH, *(grid[s * cells:(s + 1) * cells].reshape(rows, cols, bw) for s in range(2)))

    tile = 8
    def gather(source_rows, totals):
        totals = dict(totals)
        for v in range(0, cols, tile):
            for dv in range(SPAN):
                for r in source_rows:
                    source = [gpad[s, r, v + dv:v + dv + tile] for s in range(3)]
                    for u in range(rows):
                        du = r - u
                        if 0 <= du < SPAN:
                            f = du * SPAN + dv
                            at = slice(u * cols + v, u * cols + v + tile)
                            totals[u, v] = [
                                t + weights[f, s, at] * source[s] for s, t in enumerate(totals[u, v])]
        return totals

    zero = jnp.zeros((tile, bw), F32)
    totals = {(u, v): [zero] * 3 for u in range(rows) for v in range(0, cols, tile)}
    totals = gather(range(REACH, REACH + rows), totals)

    @pl.when(me == 0)
    def _():
        both_halos.wait_recv()

    for w, first in ((0, 0), (1, REACH + rows)):
        lay(first, *(halo_in[w, s].astype(F32).reshape(REACH, cols, bw) for s in range(2)))
    totals = gather(list(range(REACH)) + list(range(REACH + rows, 2 * REACH + rows)), totals)
    moved = jnp.concatenate([k[0] - k[1] for k in totals.values()] + [k[0] + k[2] for k in totals.values()], axis=0).astype(BF)
    send_b[...] = mm(back, moved).astype(BF).reshape(nd, 2 * bc, bw)
    for to in sorted(range(1, nd), key=lambda d: (reach(d), d)):
        @pl.when(me != to)
        def _():
            a, b = to // 2 // ny, to // 2 % ny
            place = slot_of(lax.rem(mz + nz - a, nz), lax.rem(my + ny - b, ny))
            pltpu.make_async_remote_copy(
                src_ref=send_b.at[to], dst_ref=recv_b.at[2 * place + mx], send_sem=phase_sem,
                recv_sem=slot_sem.at[place], device_id={"dir": to},
                device_id_type=pl.DeviceIdType.MESH).start()
    recv_b[mx] = send_b[me]
    whole(send_a, recv_a, child_sem, recv_a_sem, 0, nd - 1).wait_send()
    both_halos.wait_send()

    for j in range(slots):
        interp_t[j] = jnp.transpose(interp_v[j])

    def shifted(j):
        block = jnp.concatenate([recv_b[2 * j], recv_b[2 * j + 1]], axis=1).astype(F32)
        re = block[:bc]
        im = block[bc:]
        pieces = []
        for c in range(ch):
            cc = cos_v[j, c:c + 1]
            ss = sin_v[j, c:c + 1]
            pieces.append(cc * re + ss * im)
            pieces.append(cc * im - ss * re)
        return jnp.concatenate(pieces, axis=0).astype(BF)

    near_first = far[::-1]
    for i, j in enumerate(near_first):
        if i == slots - 1:
            whole(send_b, recv_b, phase_sem, slot_sem.at[j], 0, nd - 1).wait_send()
        whole(send_b, recv_b, phase_sem, slot_sem.at[j], 2 * j, 1 if i == 0 else 2).wait_recv()
        term = mm(shifted(j), interp_t[j])
        if i < slots - 1:
            acc_v[...] = term if i == 0 else acc_v[...] + term
        else:
            out[...] = ((acc_v[...] + term) * (dc / dp)).astype(BF)


def per_device(nd, nb, child, interp, phase, order, codes, chosen, operators):
    bc, ch, _, dc = child.shape
    dp = interp.shape[1]
    rows, cols, nlist = codes.shape
    nops, _, bw = operators.shape
    cells = rows * cols
    nz, ny = grid_of(nd)
    slots = nz * ny
    entries = SPAN * SPAN + SPAN * SPAN % 2
    lanes = ((nlist + 63) // 64) * 64
    pad_rows = ((2 * SPAN * SPAN + 15) // 16) * 16
    total = bc * ch * 2
    vmem = pl.BlockSpec(memory_space=pltpu.VMEM)
    hbm = pl.BlockSpec(memory_space=pltpu.HBM)
    result = pl.pallas_call(
        functools.partial(kernel, nd, nb, bc, ch, rows, cols),
        out_shape=jax.ShapeDtypeStruct((total, dc), BF),
        in_specs=[hbm] * 7,
        out_specs=vmem,
        scratch_shapes=[
            pltpu.VMEM(order.shape, I32),
            pltpu.VMEM((cells, nlist), I32),
            pltpu.VMEM((cells, nlist), I32),
            pltpu.VMEM((nops * 2, bw), BF),
            pltpu.VMEM((bc * ch, 2, dc), BF),
            pltpu.VMEM((slots, dc, 2 * bw), BF),
            pltpu.VMEM((ch, dp), F32),
            pltpu.VMEM((slots, ch, 2 * bw), F32),
            pltpu.VMEM((slots, ch, 2 * bw), F32),
            pltpu.VMEM((nd, 2 * bc, bw), BF),
            pltpu.VMEM((nd, 2 * bc, bw), BF),
            pltpu.VMEM((cells // 2 * pad_rows, nops), F32),
            pltpu.VMEM((SPAN * SPAN, 3, cells, bw), F32),
            pltpu.VMEM((3, rows + 2 * REACH, 24, bw), F32),
            pltpu.VMEM((2, 2, REACH * cols, bw), BF),
            pltpu.VMEM((2, 2, REACH * cols, bw), BF),
            pltpu.VMEM((nd, 2 * bc, bw), BF),
            pltpu.VMEM((nd, 2 * bc, bw), BF),
            pltpu.VMEM((total, dc), F32),
            pltpu.VMEM((slots, 2 * bw, dc), BF),
            pltpu.VMEM((3, entries * bc, bw), F32),
            pltpu.VMEM((2 * entries * bc, 2 * cells), BF),
            pltpu.VMEM((2 * entries * bc, 4 * REACH * cols), BF),
            pltpu.VMEM((2 * bc, bw), BF),
            pltpu.SemaphoreType.DMA((slots,)),
            pltpu.SemaphoreType.DMA,
            pltpu.SemaphoreType.DMA,
            pltpu.SemaphoreType.DMA,
            pltpu.SemaphoreType.DMA,
            pltpu.SemaphoreType.DMA,
            pltpu.SemaphoreType.DMA,
            pltpu.SemaphoreType.DMA,
            pltpu.SemaphoreType.DMA,
        ],
        compiler_params=pltpu.CompilerParams(
            collective_id=0, has_side_effects=True, vmem_limit_bytes=32 * 2 ** 20),
    )(*(
        pltpu.with_memory_space_constraint(value, pltpu.HBM)
        for value in (
            child.reshape(bc * ch, 2, dc), interp, phase, order,
            codes.reshape(cells, nlist), chosen.reshape(cells, nlist),
            operators.reshape(nops * 2, bw),
        )
    ))
    return result.reshape(ch, 2, bc, dc).transpose(2, 0, 1, 3)


def solution(mesh):
    in_specs = (
        P(("box", "dir"), None, None, None),
        P(),
        P(),
        P("box", None),
        P("box", None, None),
        P("box", None, None),
        P(None, None, "dir"),
    )
    out_specs = P(("box", "dir"), None, None, None)
    return jax.shard_map(
        functools.partial(per_device, mesh.shape["dir"], mesh.shape["box"]),
        mesh=mesh, in_specs=in_specs, out_specs=out_specs, check_vma=False,
    )
```

```python
import functools

import jax
import jax.numpy as jnp
from jax import lax
from jax.experimental import pallas as pl
from jax.experimental.pallas import tpu as pltpu
from jax.sharding import PartitionSpec as P

BF = jnp.bfloat16
F32 = jnp.float32
I32 = jnp.int32
REACH = 3
SPAN = 2 * REACH + 1


def onehot(mask):
    return jnp.where(mask, jnp.float32(1), jnp.float32(0))


def mm(a, b):
    return jnp.dot(a, b, preferred_element_type=F32)


SIN = (1.0, -0.16666666541438965, 0.008333329264451874, -0.00019840702862140153,
       2.751885561882994e-06, -2.3794713199798423e-08)
COS = (0.4999999954953283, -0.041666640727244325, 0.0013888403499237425,
       -2.476188584583927e-05, 2.6077099012783433e-07)


def horner(coefficients, t):
    value = jnp.full(t.shape, coefficients[-1], F32)
    for c in coefficients[-2::-1]:
        value = value * t + jnp.float32(c)
    return value


def cos_sin(angle):
    half = angle * 0.5
    t = half * half
    sine = half * horner(SIN, t)
    cosine = 1.0 - t * horner(COS, t)
    return (cosine - sine) * (cosine + sine), 2.0 * (sine * cosine)


def grid_of(nd):
    across = nd // 2
    ny = 2 if across % 2 == 0 else 1
    return across // ny, ny


def kernel(
    nd, nb, bc, ch, rows, cols,
    child, interp, phase, order, codes, chosen, ops, out,
    order_v, codes_v, chosen_v, ops_v, child_v, interp_v, phase_v, cos_v, sin_v, send_a, recv_a, cnt, weights, gpad,
    halo_out, halo_in, send_b, recv_b, acc_v, interp_t, first_w, first_in, send_first_b,
    slot_sem, recv_a_sem, halo_s_sem, halo_r_sem, child_sem, phase_sem, order_sem, codes_sem, ops_sem,
):
    dc, dp = interp.shape
    bw = ops.shape[1]
    nops = ops.shape[0] // 2
    cells = rows * cols
    pair = 2 * bw
    nz, ny = grid_of(nd)
    slots = nz * ny
    me = lax.axis_index("dir")
    mb = lax.axis_index("box")
    up = lax.rem(mb + 1, nb)
    down = lax.rem(mb + nb - 1, nb)
    mx = lax.rem(me, 2)
    mq = lax.div(me, 2)
    my = lax.rem(mq, ny)
    mz = lax.div(mq, ny)

    def hops(offset):
        return sum(min(d, n - d) for d, n in zip(offset, (nz, ny)))

    offsets = [(a, b) for a in range(nz) for b in range(ny)]
    far = sorted(range(slots), key=lambda j: (-hops(offsets[j]), -min(offsets[j][0], nz - offsets[j][0])))

    def slot_of(a, b):
        return a * ny + b

    def reach(d):
        return d // 2 // ny + d // 2 % ny + d % 2

    ahead = [lax.rem(mz + a, nz) * ny + lax.rem(my + b, ny) for a, b in offsets]
    behind = [lax.rem(mz + nz - a, nz) * ny + lax.rem(my + ny - b, ny) for a, b in offsets]

    partners = []
    for j in far:
        for flip in (1, 0):
            if j or flip:
                partners.append((j, lax.rem(mx + flip, 2), flip))

    barrier = pltpu.get_barrier_semaphore()
    for j, h, flip in partners:
        pl.semaphore_signal(barrier, inc=1, device_id={"dir": ahead[j] * 2 + h},
                            device_id_type=pl.DeviceIdType.MESH)
    edges = (up, down) if nb > 2 else (up,)
    for other in edges:
        pl.semaphore_signal(barrier, inc=1, device_id={"box": other},
                            device_id_type=pl.DeviceIdType.MESH)

    first_loads = [
        pltpu.make_async_copy(child, child_v, child_sem),
        pltpu.make_async_copy(phase, phase_v, phase_sem),
    ]
    columns = []
    for i, j in enumerate(far):
        part = pl.ds(pl.multiple_of(ahead[j] * pair, pair), pair)
        columns.append(pltpu.make_async_copy(interp.at[:, part], interp_v.at[j], slot_sem.at[i]))
    tables = [
        pltpu.make_async_copy(source, dest, sem)
        for source, dest, sem in (
            (order, order_v, order_sem), (codes, codes_v, codes_sem), (chosen, chosen_v, halo_s_sem), (ops, ops_v, ops_sem))
    ]
    for copy in first_loads + columns + tables:
        copy.start()

    group = 2 * ch
    total = bc * group
    r0 = lax.broadcasted_iota(I32, (total, total), 0)
    r1 = lax.broadcasted_iota(I32, (total, total), 1)
    bshift = bc.bit_length() - 1
    pick = onehot(r1 == (r0 & (bc - 1)) * group + (r0 >> bshift)).astype(BF)
    first_loads[0].wait()
    x = mm(pick, child_v[...].reshape(total, dc)).astype(BF)
    first_loads[1].wait()
    for j in range(slots):
        part = pl.ds(pl.multiple_of(ahead[j] * pair, pair), pair)
        cos_v[j], sin_v[j] = cos_sin(phase_v[:, part])

    def combine(j, prod):
        re = jnp.zeros((bc, pair), F32)
        im = jnp.zeros((bc, pair), F32)
        for c in range(ch):
            cc = cos_v[j, c:c + 1]
            ss = sin_v[j, c:c + 1]
            pr = prod[c * 2 * bc:c * 2 * bc + bc]
            pi = prod[c * 2 * bc + bc:(c + 1) * 2 * bc]
            re = re + (cc * pr - ss * pi)
            im = im + (cc * pi + ss * pr)
        block = jnp.concatenate([re, im], axis=0).astype(BF)
        for h in range(2):
            send_a[2 * j + h] = block[:, h * bw:(h + 1) * bw]

    def send_first(j, h):
        return pltpu.make_async_remote_copy(
            src_ref=send_a.at[2 * j + h], dst_ref=recv_a.at[me], send_sem=child_sem,
            recv_sem=recv_a_sem, device_id={"dir": ahead[j] * 2 + h},
            device_id_type=pl.DeviceIdType.MESH)

    def send_back(j, h):
        to = behind[j] * 2 + h
        return pltpu.make_async_remote_copy(
            src_ref=send_b.at[to], dst_ref=recv_b.at[2 * j + mx], send_sem=phase_sem,
            recv_sem=slot_sem.at[j], device_id={"dir": to},
            device_id_type=pl.DeviceIdType.MESH)

    def whole(source, dest, s_sem, r_sem, first, count):
        part = pl.ds(first, count)
        return pltpu.make_async_remote_copy(
            src_ref=source.at[part], dst_ref=dest.at[part], send_sem=s_sem, recv_sem=r_sem,
            device_id={"dir": me}, device_id_type=pl.DeviceIdType.MESH)

    last = None
    for i, j in enumerate(far):
        columns[i].wait()
        prod = mm(x, interp_v[j])
        if last is not None:
            combine(far[i - 1], last)
        last = prod
    combine(0, last)

    pl.semaphore_wait(barrier, nd - 1 + len(edges))
    for to in sorted(range(nd), key=lambda d: (-reach(d), -d)):
        @pl.when(me != to)
        def _():
            a, b = to // 2 // ny, to // 2 % ny
            place = slot_of(lax.rem(a + nz - mz, nz), lax.rem(b + ny - my, ny))
            pltpu.make_async_remote_copy(
                src_ref=send_a.at[2 * place + to % 2], dst_ref=recv_a.at[me], send_sem=child_sem,
                recv_sem=recv_a_sem, device_id={"dir": to},
                device_id_type=pl.DeviceIdType.MESH).start()
    recv_a[me] = send_a[mx]

    for copy in tables:
        copy.wait()

    q0 = lax.broadcasted_iota(I32, (2 * cells, 2 * cells), 0)
    listed = order_v[...]
    slot = (listed >> bshift) * (2 * bc) + (listed & (bc - 1))
    back = onehot(q0 == jnp.concatenate([slot, slot + bc], axis=1))
    place = jnp.transpose(back).astype(BF)
    back = back.astype(BF)

    o0 = lax.broadcasted_iota(I32, (nops, 2 * nops), 0)
    o1 = lax.broadcasted_iota(I32, (nops, 2 * nops), 1)
    raw = ops_v[...]
    table = jnp.concatenate(
        [mm(onehot(o1 == 2 * o0 + s).astype(BF), raw).astype(BF) for s in range(2)], axis=1)

    half = cells // 2
    nlist = codes.shape[1]
    lanes = ((nlist + 63) // 64) * 64
    fill = jnp.full((half, lanes - nlist), -1, I32)
    code = codes_v[...]
    picked = chosen_v[...]
    both_codes = jnp.concatenate(
        [code[:half], fill, code[half:] + SPAN * SPAN, fill], axis=1)
    both_ops = jnp.concatenate([picked[:half], fill, picked[half:], fill], axis=1)
    span_rows = 2 * SPAN * SPAN
    pad_rows = ((span_rows + 15) // 16) * 16
    m0 = lax.broadcasted_iota(I32, (pad_rows, 2 * lanes), 0)
    n0 = lax.broadcasted_iota(I32, (nops, 2 * lanes), 0)
    for g in range(half):
        left = onehot(m0 == both_codes[g:g + 1]).astype(BF)
        right = onehot(n0 == both_ops[g:g + 1]).astype(BF)
        cnt[g * pad_rows:(g + 1) * pad_rows] = lax.dot_general(
            left, right, (((1,), (1,)), ((), ())), preferred_element_type=F32)
    for f in range(SPAN * SPAN):
        both = jnp.concatenate(
            [cnt[pl.ds(c * SPAN * SPAN + f, half, stride=pad_rows)] for c in range(2)],
            axis=0).astype(BF)
        weight = mm(both, table)
        wr, wi = weight[:, :bw], weight[:, bw:]
        weights[f, 0] = wr
        weights[f, 1] = wr + wi
        weights[f, 2] = wi - wr

    edge = REACH * cols
    spans = SPAN * SPAN
    entries = spans + spans % 2

    def prepare_first():
        cshift = cols.bit_length() - 1
        held = onehot(listed == lax.broadcasted_iota(I32, (bc, cells), 0))
        cell = lax.broadcasted_iota(I32, (bc, cells), 1)
        home_u = jnp.sum(held * (cell >> cshift).astype(F32), axis=1, keepdims=True).astype(I32)
        home_v = jnp.sum(held * (cell & (cols - 1)).astype(F32), axis=1, keepdims=True).astype(I32)
        held = held.astype(BF)
        none = jnp.full((bc, lanes - nlist), -1, I32)
        own_code = jnp.concatenate([mm(held, code.astype(F32).astype(BF)).astype(I32), none], axis=1)
        own_ops = jnp.concatenate([mm(held, picked.astype(F32).astype(BF)).astype(I32), none], axis=1)
        box_rows = ((spans + 15) // 16) * 16
        m1 = lax.broadcasted_iota(I32, (box_rows, lanes), 0)
        n1 = lax.broadcasted_iota(I32, (nops, lanes), 0)
        for g in range(bc):
            left = onehot(m1 == own_code[g:g + 1]).astype(BF)
            right = onehot(n1 == own_ops[g:g + 1]).astype(BF)
            cnt[g * box_rows:(g + 1) * box_rows] = lax.dot_general(
                left, right, (((1,), (1,)), ((), ())), preferred_element_type=F32)
        times = [cnt[pl.ds(f, bc, stride=box_rows)] for f in range(spans)]
        times += [jnp.zeros((bc, nops), F32)] * (entries - spans)
        weight = mm(jnp.concatenate(times, axis=0).astype(BF), table)
        wr, wi = weight[:, :bw], weight[:, bw:]
        first_w[0] = wr
        first_w[1] = wr + wi
        first_w[2] = wi - wr

        lane = lax.broadcasted_iota(I32, (bc, cells), 1)
        halo_lane = lax.broadcasted_iota(I32, (bc, 4 * edge), 1)
        wide_u = jnp.broadcast_to(home_u, (bc, 4 * edge))
        wide_v = jnp.broadcast_to(home_v, (bc, 4 * edge))
        inside, beyond = [], [[], []]
        for f in range(entries):
            r = wide_u + (f // SPAN - REACH)
            at = r * cols + ((wide_v + (f % SPAN - REACH)) & (cols - 1))
            inside.append(onehot(at[:, :cells] == lane))
            past = jnp.where(r < 0, at + edge, jnp.where(r >= rows, at - cells + 2 * edge, -4 * edge))
            for s in range(2):
                beyond[s].append(onehot(past + s * edge == halo_lane))
        inside = jnp.concatenate(inside, axis=0).astype(BF)
        for s in range(2):
            part = slice(s * entries * bc, (s + 1) * entries * bc)
            first_in[part, :2 * cells] = mm(inside, place[s * cells:(s + 1) * cells]).astype(BF)
            first_in[part, 2 * cells:] = jnp.concatenate(beyond[s], axis=0).astype(BF)

    late_core = lax.rem(mb, 2)
    pl.when(late_core == 0)(prepare_first)

    whole(send_a, recv_a, child_sem, recv_a_sem, 0, nd - 1).wait_recv()
    grid = mm(place, recv_a[...].reshape(2 * cells, bw))
    for s in range(2):
        halo_out[0, s] = grid[(s + 1) * cells - edge:(s + 1) * cells].astype(BF)
        halo_out[1, s] = grid[s * cells:s * cells + edge].astype(BF)
    halos = [
        pltpu.make_async_remote_copy(
            src_ref=halo_out.at[w], dst_ref=halo_in.at[w], send_sem=halo_s_sem,
            recv_sem=halo_r_sem, device_id={"box": other},
            device_id_type=pl.DeviceIdType.MESH)
        for w, other in ((0, up), (1, down))
    ]
    for copy in halos:
        copy.start()
    pl.when(late_core != 0)(prepare_first)
    both_halos = pltpu.make_async_remote_copy(
        src_ref=halo_out, dst_ref=halo_in, send_sem=halo_s_sem, recv_sem=halo_r_sem,
        device_id={"box": mb}, device_id_type=pl.DeviceIdType.MESH)

    @pl.when(me != 0)
    def _():
        both_halos.wait_recv()
        found = mm(first_in[...], jnp.concatenate(
            [recv_a[...].reshape(2 * cells, bw), halo_in[...].reshape(4 * edge, bw)], axis=0))
        sums = [jnp.zeros((bc, bw), F32)] * 3
        for f in range(spans):
            re = found[f * bc:(f + 1) * bc]
            im = found[(entries + f) * bc:(entries + f + 1) * bc]
            sums = [t + first_w[s, f * bc:(f + 1) * bc] * z for s, (t, z) in enumerate(zip(sums, (re + im, im, re)))]
        send_first_b[...] = jnp.concatenate([sums[0] - sums[1], sums[0] + sums[2]], axis=0).astype(BF)
        slot = slot_of(mz, my)
        pltpu.make_async_remote_copy(
            src_ref=send_first_b, dst_ref=recv_b.at[2 * slot + mx], send_sem=phase_sem,
            recv_sem=slot_sem.at[slot], device_id={"dir": 0},
            device_id_type=pl.DeviceIdType.MESH).start()

    def lay(first, re, im):
        count = re.shape[0]
        for s, values in enumerate((re + im, im, re)):
            gpad[s, first:first + count, REACH:REACH + cols] = values
            gpad[s, first:first + count, 0:REACH] = values[:, cols - REACH:]
            gpad[s, first:first + count, REACH + cols:2 * REACH + cols] = values[:, :REACH]

    lay(REACH, *(grid[s * cells:(s + 1) * cells].reshape(rows, cols, bw) for s in range(2)))

    tile = 8
    def gather(source_rows, totals):
        totals = dict(totals)
        for v in range(0, cols, tile):
            for dv in range(SPAN):
                for r in source_rows:
                    source = [gpad[s, r, v + dv:v + dv + tile] for s in range(3)]
                    for u in range(rows):
                        du = r - u
                        if 0 <= du < SPAN:
                            f = du * SPAN + dv
                            at = slice(u * cols + v, u * cols + v + tile)
                            totals[u, v] = [
                                t + weights[f, s, at] * source[s] for s, t in enumerate(totals[u, v])]
        return totals

    zero = jnp.zeros((tile, bw), F32)
    totals = {(u, v): [zero] * 3 for u in range(rows) for v in range(0, cols, tile)}
    totals = gather(range(REACH, REACH + rows), totals)

    @pl.when(me == 0)
    def _():
        both_halos.wait_recv()

    for w, first in ((0, 0), (1, REACH + rows)):
        lay(first, *(halo_in[w, s].astype(F32).reshape(REACH, cols, bw) for s in range(2)))
    totals = gather(list(range(REACH)) + list(range(REACH + rows, 2 * REACH + rows)), totals)
    moved = jnp.concatenate([k[0] - k[1] for k in totals.values()] + [k[0] + k[2] for k in totals.values()], axis=0).astype(BF)
    send_b[...] = mm(back, moved).astype(BF).reshape(nd, 2 * bc, bw)
    for to in sorted(range(1, nd), key=lambda d: (reach(d), d)):
        @pl.when(me != to)
        def _():
            a, b = to // 2 // ny, to // 2 % ny
            place = slot_of(lax.rem(mz + nz - a, nz), lax.rem(my + ny - b, ny))
            pltpu.make_async_remote_copy(
                src_ref=send_b.at[to], dst_ref=recv_b.at[2 * place + mx], send_sem=phase_sem,
                recv_sem=slot_sem.at[place], device_id={"dir": to},
                device_id_type=pl.DeviceIdType.MESH).start()
    recv_b[mx] = send_b[me]
    whole(send_a, recv_a, child_sem, recv_a_sem, 0, nd - 1).wait_send()
    both_halos.wait_send()

    for j in range(slots):
        interp_t[j] = jnp.transpose(interp_v[j])

    def shifted(j):
        block = jnp.concatenate([recv_b[2 * j], recv_b[2 * j + 1]], axis=1).astype(F32)
        re = block[:bc]
        im = block[bc:]
        pieces = []
        for c in range(ch):
            cc = cos_v[j, c:c + 1]
            ss = sin_v[j, c:c + 1]
            pieces.append(cc * re + ss * im)
            pieces.append(cc * im - ss * re)
        return jnp.concatenate(pieces, axis=0).astype(BF)

    near_first = far[::-1]
    for i, j in enumerate(near_first):
        whole(send_b, recv_b, phase_sem, slot_sem.at[j], 2 * j, 1 if i == 0 else 2).wait_recv()
        term = mm(shifted(j), interp_t[j])
        if i < slots - 1:
            acc_v[...] = term if i == 0 else acc_v[...] + term
        else:
            out[...] = ((acc_v[...] + term) * (dc / dp)).astype(BF)
    whole(send_b, recv_b, phase_sem, slot_sem.at[0], 0, nd - 1).wait_send()


def per_device(nd, nb, child, interp, phase, order, codes, chosen, operators):
    bc, ch, _, dc = child.shape
    dp = interp.shape[1]
    rows, cols, nlist = codes.shape
    nops, _, bw = operators.shape
    cells = rows * cols
    nz, ny = grid_of(nd)
    slots = nz * ny
    entries = SPAN * SPAN + SPAN * SPAN % 2
    lanes = ((nlist + 63) // 64) * 64
    pad_rows = ((2 * SPAN * SPAN + 15) // 16) * 16
    total = bc * ch * 2
    vmem = pl.BlockSpec(memory_space=pltpu.VMEM)
    hbm = pl.BlockSpec(memory_space=pltpu.HBM)
    result = pl.pallas_call(
        functools.partial(kernel, nd, nb, bc, ch, rows, cols),
        out_shape=jax.ShapeDtypeStruct((total, dc), BF),
        in_specs=[hbm] * 7,
        out_specs=vmem,
        scratch_shapes=[
            pltpu.VMEM(order.shape, I32),
            pltpu.VMEM((cells, nlist), I32),
            pltpu.VMEM((cells, nlist), I32),
            pltpu.VMEM((nops * 2, bw), BF),
            pltpu.VMEM((bc * ch, 2, dc), BF),
            pltpu.VMEM((slots, dc, 2 * bw), BF),
            pltpu.VMEM((ch, dp), F32),
            pltpu.VMEM((slots, ch, 2 * bw), F32),
            pltpu.VMEM((slots, ch, 2 * bw), F32),
            pltpu.VMEM((nd, 2 * bc, bw), BF),
            pltpu.VMEM((nd, 2 * bc, bw), BF),
            pltpu.VMEM((cells // 2 * pad_rows, nops), F32),
            pltpu.VMEM((SPAN * SPAN, 3, cells, bw), F32),
            pltpu.VMEM((3, rows + 2 * REACH, 24, bw), F32),
            pltpu.VMEM((2, 2, REACH * cols, bw), BF),
            pltpu.VMEM((2, 2, REACH * cols, bw), BF),
            pltpu.VMEM((nd, 2 * bc, bw), BF),
            pltpu.VMEM((nd, 2 * bc, bw), BF),
            pltpu.VMEM((total, dc), F32),
            pltpu.VMEM((slots, 2 * bw, dc), BF),
            pltpu.VMEM((3, entries * bc, bw), F32),
            pltpu.VMEM((2 * entries * bc, 2 * cells + 4 * REACH * cols), BF),
            pltpu.VMEM((2 * bc, bw), BF),
            pltpu.SemaphoreType.DMA((slots,)),
            pltpu.SemaphoreType.DMA,
            pltpu.SemaphoreType.DMA,
            pltpu.SemaphoreType.DMA,
            pltpu.SemaphoreType.DMA,
            pltpu.SemaphoreType.DMA,
            pltpu.SemaphoreType.DMA,
            pltpu.SemaphoreType.DMA,
            pltpu.SemaphoreType.DMA,
        ],
        compiler_params=pltpu.CompilerParams(
            collective_id=0, has_side_effects=True, vmem_limit_bytes=32 * 2 ** 20),
    )(*(
        pltpu.with_memory_space_constraint(value, pltpu.HBM)
        for value in (
            child.reshape(bc * ch, 2, dc), interp, phase, order,
            codes.reshape(cells, nlist), chosen.reshape(cells, nlist),
            operators.reshape(nops * 2, bw),
        )
    ))
    return result.reshape(ch, 2, bc, dc).transpose(2, 0, 1, 3)


def solution(mesh):
    in_specs = (
        P(("box", "dir"), None, None, None),
        P(),
        P(),
        P("box", None),
        P("box", None, None),
        P("box", None, None),
        P(None, None, "dir"),
    )
    out_specs = P(("box", "dir"), None, None, None)
    return jax.shard_map(
        functools.partial(per_device, mesh.shape["dir"], mesh.shape["box"]),
        mesh=mesh, in_specs=in_specs, out_specs=out_specs, check_vma=False,
    )
```
